256 devices in a mesh: panel: 16 (over z, y_hi), mic: 8 (over x, core), tm: 2 (over y_lo).
Axes of the slice: x: 4, y: 4 (y_hi: 2, y_lo: 2; y = y_hi * 2 + y_lo), z: 8, core: 2. Of those that a mesh axis runs over, the one named last changes fastest.
Arguments:
- sources: bfloat16 [16384, 8, 256], P('panel', None, 'tm'), may hold values from -6 to 6
- transfer_matrix: bfloat16 [4096, 16384], P('mic', 'panel'), may hold values from -0.046875 to 0.046875
- delay_groups: int32 [128, 32], P('panel', 'mic'), may hold values from 0 to 32
- patch_block: int32 [128], P('panel'), may hold values from 0 to 127, as said below
Outputs:
- normal_product: bfloat16 [16384, 8, 256], P(('panel', 'mic'), None, 'tm')
The draws below stay inside these ranges and needn't reach their ends.
Inputs may be any that keep to these rules, and one draw needn't show every extreme that they name: No two patches share a value, and patch q's value lies in the same run of 8 blocks as q itself (q // 8 == patch_block[q] // 8).
All inputs are finite; a program needn't handle non-finite values.
Results may differ from the reference program's by a relative error of at most 0.017.
Values may be sent and summed in bfloat16 or wider, within the bound.
A program may use at most 64 MiB of HBM per device.

```python
import jax
import jax.numpy as jnp
from jax import lax

W = 256
DMAX = 32
PATCH = 128
MB = 128
NVEC = 8
P_SIZE = 16384
M = 4096
PATCH_DEV = 8
NPATCH = 128
NMB = 32
NMB_DEV = 4
N_PANEL = 16
N_MIC = 8


def draw_patch_block(key, part):
    device_keys = jax.random.split(key, N_PANEL)
    orders = jax.vmap(lambda single_key: jax.random.permutation(single_key, PATCH_DEV))(device_keys)
    offsets = jnp.arange(N_PANEL, dtype=jnp.int32)[:, None] * PATCH_DEV
    return (orders.astype(jnp.int32) + offsets).reshape(-1).astype(jnp.int32)


def plant(drawn, stream_key, least, high):
    shape = drawn.shape
    index_at = [jax.random.randint(jax.random.fold_in(stream_key, axis), (), 0, shape[axis]) for axis in range(len(shape))]
    drawn = drawn.at[tuple(index_at)].set(least)
    longest = shape.index(max(shape))
    index_at[longest] = (index_at[longest] + 1) % shape[longest]
    return drawn.at[tuple(index_at)].set(high)


def block_levels(own_key, dims, pieces, smallest, largest):
    def one(dim, blocks):
        heights = jax.random.uniform(jax.random.fold_in(jax.random.fold_in(own_key, 6), dim), (blocks,), jnp.float32, smallest / len(pieces), largest / len(pieces))
        return jnp.repeat(jnp.exp(heights), dims[dim] // blocks).reshape((-1,) + (1,) * (len(dims) - dim - 1))

    loudness = one(*pieces[0])
    for cut in pieces[1:]:
        loudness = loudness * one(*cut)
    return loudness


def centred(own_key, dims, spread, bound, pieces=(), held_as=jnp.bfloat16):
    values = spread * jax.random.normal(own_key, dims, jnp.float32)
    if pieces:
        values = values * block_levels(own_key, dims, pieces, -0.22, 0.18)
    return jnp.clip(values, -bound, bound).astype(held_as)


def setup_inputs(seed: int = 0) -> dict:
    seeds = jax.random.split(jax.random.key(seed), 5)
    return {
        "sources": centred(seeds[0], (P_SIZE, NVEC, W), 1.0, 6.0, ((0, 16), (2, 2))),
        "transfer_matrix": centred(seeds[1], (M, P_SIZE), P_SIZE ** -0.5, 0.046875, ((0, 8), (1, 16))),
        "delay_groups": plant(jax.random.randint(seeds[2], (NPATCH, NMB), 0, DMAX + 1), jax.random.fold_in(seeds[2], 1), 0, DMAX).astype(jnp.int32),
        "patch_block": draw_patch_block(jax.random.fold_in(seeds[4], 71), 0),
    }


def shift_slabs(slabs, offsets, length):
    def one_slab(single_slab, offset_value):
        return lax.dynamic_slice_in_dim(single_slab, offset_value, length, axis=2)
    return jax.vmap(one_slab)(slabs, offsets)


def reference(sources, transfer_matrix, delay_groups, patch_block):
    length = W + DMAX
    extended = jnp.pad(sources, ((0, 0), (0, 0), (DMAX, 0)))
    in_patches = extended.reshape(NPATCH, PATCH, NVEC, length)[patch_block]

    def forward(mic_block):
        delays = lax.dynamic_index_in_dim(delay_groups, mic_block, 1, False)
        shifted = shift_slabs(in_patches, DMAX - delays, W).reshape(P_SIZE, NVEC, W).astype(jnp.float32)
        weights = lax.dynamic_slice_in_dim(transfer_matrix, mic_block * MB, MB, 0).astype(jnp.float32)
        return jnp.einsum("mp,pnt->mnt", weights, shifted)

    pressure = lax.map(forward, jnp.arange(NMB, dtype=jnp.int32)).reshape(M, NVEC, W).astype(jnp.bfloat16)
    padded = jnp.pad(pressure, ((0, 0), (0, 0), (0, DMAX)))
    zeros = jnp.zeros((NPATCH, PATCH, NVEC, W), jnp.float32)

    def group_sum(total, group):
        def block_sum(partial_value, inner):
            mic_block = group * NMB_DEV + inner
            rows = lax.dynamic_slice_in_dim(padded, mic_block * MB, MB, 0)
            delays = lax.dynamic_index_in_dim(delay_groups, mic_block, 1, False)

            def advance(offset_value):
                return lax.dynamic_slice_in_dim(rows, offset_value, W, axis=2)

            shifted = jax.vmap(advance)(delays).astype(jnp.float32)
            weights = lax.dynamic_slice_in_dim(transfer_matrix, mic_block * MB, MB, 0)
            weights = weights.reshape(MB, NPATCH, PATCH).astype(jnp.float32)
            return partial_value + jnp.einsum("mqp,qmnt->qpnt", weights, shifted), None

        partial_value, _ = lax.scan(block_sum, zeros, jnp.arange(NMB_DEV, dtype=jnp.int32))
        rounded = lax.optimization_barrier(partial_value.astype(jnp.bfloat16)).astype(jnp.float32)
        return total + rounded, None

    total, _ = lax.scan(group_sum, zeros, jnp.arange(N_MIC, dtype=jnp.int32))
    order = jnp.argsort(patch_block).astype(jnp.int32)
    return total[order].reshape(P_SIZE, NVEC, W).astype(jnp.bfloat16)
```

```python
import jax
import jax.numpy as jnp
from jax import lax
from jax.experimental import pallas as pl
from jax.experimental.pallas import tpu as pltpu
from jax.sharding import PartitionSpec as P

DMAX = 32
PATCH = 128
MB = 128
NVEC = 8
NZ = 8
NX = 4
CH = 32
ROWS = CH // NZ
HALF = ROWS // 2
MESH = pl.DeviceIdType.MESH
F32 = jnp.float32
BF16 = jnp.bfloat16


def reorder(dg_ref, pb_ref, mat, delays, tiles):
    patches, blocks = dg_ref.shape
    base = lax.axis_index("panel") * patches
    for j in range(patches):
        owner = jnp.int32(0)
        for q in range(patches):
            owner = owner + jnp.where(pb_ref[q] - base == j, q, 0)
        for b in range(blocks):
            delays[j * blocks + b] = dg_ref[owner, b]
        cols = pl.ds(pl.multiple_of(owner * PATCH, PATCH), PATCH)
        tiles[:, j * PATCH : (j + 1) * PATCH] = mat[:, cols]


def body(
    delays, src_hbm, mat_hbm, out_ref,
    sbuf, tiles, fa, fb, st, part, rs_recv, rs_send, y_send, y_recv, o_recv, gath, work,
    g_send, g_keep, g_recv, x0_send, x0_recv, x1_send, x1_recv, fin,
    in_sem, rs_ss, rs_rs, y_ss, y_rs, o_ss, o_rs, ag_ss, ag_rs, c_ss, c_rs, x0_ss, x0_rs, x1_ss, x1_rs,
):
    panel_dev, nvec, half = sbuf.shape
    patches = panel_dev // PATCH
    blocks = tiles.shape[0] // MB
    panel, mic, tm = (lax.axis_index(name) for name in ("panel", "mic", "tm"))
    z, y_hi = panel // 2, panel % 2
    x, core = mic // 2, mic % 2

    def z_at(step):
        return (z + step + NZ) % NZ

    def x_at(step):
        return (x + step + NX) % NX

    def z_peer(sign):
        return {"panel": z_at(sign) * 2 + y_hi}

    def x_peer(sign):
        return {"mic": x_at(sign) * 2 + core}

    y_peer = {"panel": z * 2 + 1 - y_hi}
    o_peers = ({"tm": 1 - tm}, {"panel": z * 2 + 1 - y_hi, "tm": 1 - tm})
    core_peer = {"mic": x * 2 + 1 - core}
    signs = (1, -1)

    barrier = pltpu.get_barrier_semaphore()
    peers = [z_peer(1), z_peer(-1), y_peer, *o_peers, core_peer, x_peer(1), x_peer(-1)]
    for peer in peers:
        pl.semaphore_signal(barrier, inc=1, device_id=peer, device_id_type=MESH)

    def load_src(j):
        return pltpu.make_async_copy(
            src_hbm.at[pl.ds(j * PATCH, PATCH)], sbuf.at[pl.ds(j * PATCH, PATCH)], in_sem.at[j]
        )

    load_mat = pltpu.make_async_copy(mat_hbm, tiles, in_sem.at[patches])
    for j in range(patches):
        load_src(j).start()
    load_mat.start()

    st[0:CH] = jnp.zeros((CH,) + st.shape[1:], st.dtype)
    st[half + CH : half + 2 * CH] = jnp.zeros((CH,) + st.shape[1:], st.dtype)
    work[half : half + CH] = jnp.zeros((CH,) + work.shape[1:], work.dtype)

    @pl.loop(0, patches)
    def _(j):
        load_src(j).wait()
        fa[...] = sbuf[pl.ds(j * PATCH, PATCH)].astype(F32).reshape(PATCH * nvec, half)
        for n in range(nvec):
            fb[pl.ds(n, half, stride=nvec), :] = fa[pl.ds(n, PATCH, stride=nvec), :].T
        st[CH : CH + half, :, pl.ds(pl.multiple_of(j * PATCH, PATCH), PATCH)] = (
            fb[...].reshape(half, nvec, PATCH).astype(st.dtype)
        )

    load_mat.wait()

    pl.semaphore_wait(barrier, len(peers))

    count = jnp.where(tm == 0, 5, 4)

    def chunk_of(p):
        return jnp.where(tm == 0, 4 - p, p)

    def out_chunk(q):
        return jnp.where(tm == 0, 3 - q, q)

    def cut(way):
        return pl.ds(way * HALF, HALF)

    def rs_copy(way, step, p):
        if step == 0:
            source = part.at[chunk_of(p), z_at(4), cut(way)]
            target = rs_recv.at[way, 0, p, cut(way)]
        else:
            source = rs_send.at[way, step - 1, p]
            target = rs_recv.at[way, step, p]
        return pltpu.make_async_remote_copy(
            src_ref=source, dst_ref=target, send_sem=rs_ss.at[way, step, p], recv_sem=rs_rs.at[way, step, p],
            device_id=z_peer(signs[way]), device_id_type=MESH,
        )

    def y_copy(p):
        return pltpu.make_async_remote_copy(
            src_ref=y_send.at[p], dst_ref=y_recv.at[p], send_sem=y_ss.at[p], recv_sem=y_rs.at[p],
            device_id=y_peer, device_id_type=MESH,
        )

    def o_copy(which):
        return pltpu.make_async_remote_copy(
            src_ref=y_send.at[0], dst_ref=o_recv.at[which], send_sem=o_ss.at[which], recv_sem=o_rs.at[which],
            device_id=o_peers[which], device_id_type=MESH,
        )

    def ag_copy(way, step, p):
        owner = z_at(-signs[way] * step)
        ref = gath.at[p, owner, cut(way)] if step == 3 else gath.at[p, owner]
        return pltpu.make_async_remote_copy(
            src_ref=ref, dst_ref=ref, send_sem=ag_ss.at[way, step, p], recv_sem=ag_rs.at[way, step, p],
            device_id=z_peer(signs[way]), device_id_type=MESH,
        )

    def core_copy(q):
        return pltpu.make_async_remote_copy(
            src_ref=g_send.at[q], dst_ref=g_recv.at[q], send_sem=c_ss.at[q], recv_sem=c_rs.at[q],
            device_id=core_peer, device_id_type=MESH,
        )

    def x0_copy(way, q):
        return pltpu.make_async_remote_copy(
            src_ref=x0_send.at[way, q], dst_ref=x0_recv.at[way, q], send_sem=x0_ss.at[way, q],
            recv_sem=x0_rs.at[way, q], device_id=x_peer(signs[way]), device_id_type=MESH,
        )

    def x1_copy(way, q):
        return pltpu.make_async_remote_copy(
            src_ref=x1_send.at[way, q], dst_ref=x1_recv.at[way, q], send_sem=x1_ss.at[way, q],
            recv_sem=x1_rs.at[way, q], device_id=x_peer(signs[way]), device_id_type=MESH,
        )

    def forward(p):
        c = chunk_of(p)
        for b in range(blocks):
            pieces = []
            for j in range(patches):
                rows = pl.ds(CH * c + CH - delays[j * blocks + b], CH)
                pieces.append(st[rows, :, j * PATCH : (j + 1) * PATCH].reshape(CH * nvec, PATCH))
            acc = lax.dot_general(
                jnp.concatenate(pieces, axis=1), tiles[b * MB : (b + 1) * MB, :],
                (((1,), (1,)), ((), ())), preferred_element_type=F32,
            )
            part[c, :, :, :, b * MB : (b + 1) * MB] = acc.reshape(NZ, ROWS, nvec, MB).astype(BF16)
        for way in range(2):
            rs_copy(way, 0, p).start()

    def reduce_step(step, p):
        c = chunk_of(p)
        for way in range(2):
            rs_copy(way, step - 1, p).wait_recv()
            dest = z_at(signs[way] * (4 - step))
            if step == 1:
                here, there = cut(way), cut(1 - way)
                rs_send[way, 0, p, here] = (
                    part[c, dest, here].astype(F32) + rs_recv[way, 0, p, here].astype(F32)
                ).astype(BF16)
                rs_send[way, 0, p, there] = part[c, dest, there]
            else:
                rs_send[way, step - 1, p] = (
                    part[c, dest].astype(F32) + rs_recv[way, step - 1, p].astype(F32)
                ).astype(BF16)
            rs_copy(way, step, p).start()

    def own_sum(p):
        return (
            part[chunk_of(p), z].astype(F32) + rs_recv[0, 3, p].astype(F32) + rs_recv[1, 3, p].astype(F32)
        )

    def reduce_last(p):
        for way in range(2):
            rs_copy(way, 3, p).wait_recv()
        y_send[p] = own_sum(p).astype(BF16)
        y_copy(p).start()

        @pl.when(p == 0)
        def _():
            for which in range(2):
                o_copy(which).start()

    def gather_first(p):
        y_copy(p).wait_recv()
        total = own_sum(p) + y_recv[p].astype(F32)

        @pl.when(p == 0)
        def _():
            for which in range(2):
                o_copy(which).wait_recv()
            gath[p, z] = (total + o_recv[0].astype(F32) + o_recv[1].astype(F32)).astype(BF16)

        @pl.when(p != 0)
        def _():
            gath[p, z] = total.astype(BF16)

        for way in range(2):
            ag_copy(way, 0, p).start()

    def gather_step(step, p):
        for way in range(2):
            ag_copy(way, step - 1, p).wait_recv()
            ag_copy(way, step, p).start()

    def gather_last(p):
        for way in range(2):
            ag_copy(way, 3, p).wait_recv()
        work[pl.ds(chunk_of(p) * CH, CH)] = gath[p].reshape(CH, nvec, blocks * MB)

    def backward(q):
        start = out_chunk(q) * CH
        for target, side in ((g_send, 1 - core), (g_keep, core)):

            @pl.loop(0, NX)
            def _(k):
                j = 2 * k + side
                pieces = []
                for b in range(blocks):
                    rows = pl.ds(start + delays[j * blocks + b], CH)
                    pieces.append(work[rows, :, b * MB : (b + 1) * MB].reshape(CH * nvec, MB))
                acc = jnp.dot(
                    jnp.concatenate(pieces, axis=1), tiles[:, pl.ds(pl.multiple_of(j * PATCH, PATCH), PATCH)],
                    preferred_element_type=F32,
                )
                target[q, k] = acc.reshape(CH, nvec, PATCH).astype(BF16)

            if target is g_send:
                core_copy(q).start()

    hx = CH // 2

    def pair(q, dest, rows):
        return g_keep[q, dest, rows].astype(F32) + g_recv[q, dest, rows].astype(F32)

    def scatter_first(q):
        core_copy(q).wait_recv()
        for way in range(2):
            x0_send[way, q] = pair(q, x_at(2), pl.ds(way * hx, hx)).astype(BF16)
            x0_copy(way, q).start()

    def scatter_second(q):
        for way in range(2):
            x0_copy(way, q).wait_recv()
            dest = x_at(signs[way])
            here, there = pl.ds(way * hx, hx), pl.ds((1 - way) * hx, hx)
            x1_send[way, q, here] = (pair(q, dest, here) + x0_recv[way, q].astype(F32)).astype(BF16)
            x1_send[way, q, there] = pair(q, dest, there).astype(BF16)
            x1_copy(way, q).start()

    def scatter_last(q):
        for way in range(2):
            x1_copy(way, q).wait_recv()
        total = pair(q, x, pl.ds(0, CH)) + x1_recv[0, q].astype(F32) + x1_recv[1, q].astype(F32)
        fin[pl.ds(out_chunk(q) * CH * nvec, CH * nvec), :] = total.reshape(CH * nvec, PATCH)

    def at(i, offset, limit, step):
        @pl.when((i >= offset) & (i < offset + limit))
        def _():
            step(i - offset)

    @pl.loop(0, 17)
    def _(i):
        at(i, 13, 4, scatter_last)
        at(i, 12, 4, scatter_second)
        at(i, 11, 4, scatter_first)
        for step in (3, 2, 1):
            at(i, 5 + step, count, lambda p, step=step: gather_step(step, p))
        at(i, 5, count, gather_first)
        at(i, 4, count, reduce_last)
        for step in (3, 2, 1):
            at(i, step, count, lambda p, step=step: reduce_step(step, p))
        at(i, 0, count, forward)
        at(i, 9, count, gather_last)
        at(i, 10, 4, backward)

    for n in range(nvec):
        fb[pl.ds(n, PATCH, stride=nvec), :] = fin[pl.ds(n, half, stride=nvec), :].T
    out_ref[...] = fb[...].reshape(PATCH, nvec, half).astype(BF16)

    for which in range(2):
        o_copy(which).wait_send()

    @pl.loop(0, count)
    def _(p):
        y_copy(p).wait_send()
        for way in range(2):
            for step in range(4):
                rs_copy(way, step, p).wait_send()
                ag_copy(way, step, p).wait_send()

    @pl.loop(0, 4)
    def _(q):
        core_copy(q).wait_send()
        for way in range(2):
            x0_copy(way, q).wait_send()
            x1_copy(way, q).wait_send()


def per_device(sources, transfer_matrix, delay_groups, patch_block):
    panel_dev, nvec, half = sources.shape
    mic_dev = transfer_matrix.shape[0]
    patches, blocks = delay_groups.shape
    vm = pltpu.VMEM
    dma = pltpu.SemaphoreType.DMA
    scratch = [
        vm((panel_dev, nvec, half), BF16),
        vm((mic_dev, panel_dev), BF16),
        vm((PATCH * nvec, half), F32),
        vm((half * nvec, PATCH), F32),
        vm((half + 2 * CH, nvec, panel_dev), BF16),
        vm((5, NZ, ROWS, nvec, mic_dev), BF16),
        vm((2, 4, 5, ROWS, nvec, mic_dev), BF16),
        vm((2, 3, 5, ROWS, nvec, mic_dev), BF16),
        vm((5, ROWS, nvec, mic_dev), BF16),
        vm((5, ROWS, nvec, mic_dev), BF16),
        vm((2, ROWS, nvec, mic_dev), BF16),
        vm((5, NZ, ROWS, nvec, mic_dev), BF16),
        vm((half + CH, nvec, mic_dev), BF16),
        vm((4, NX, CH, nvec, PATCH), BF16),
        vm((4, NX, CH, nvec, PATCH), BF16),
        vm((4, NX, CH, nvec, PATCH), BF16),
        vm((2, 4, CH // 2, nvec, PATCH), BF16),
        vm((2, 4, CH // 2, nvec, PATCH), BF16),
        vm((2, 4, CH, nvec, PATCH), BF16),
        vm((2, 4, CH, nvec, PATCH), BF16),
        vm((half * nvec, PATCH), F32),
        dma((patches + 1,)),
        dma((2, 4, 5)), dma((2, 4, 5)),
        dma((5,)), dma((5,)),
        dma((2,)), dma((2,)),
        dma((2, 4, 5)), dma((2, 4, 5)),
        dma((4,)), dma((4,)),
        dma((2, 4)), dma((2, 4)),
        dma((2, 4)), dma((2, 4)),
    ]
    delays, tiles = pl.pallas_call(
        reorder,
        out_shape=(
            jax.ShapeDtypeStruct((patches * blocks,), jnp.int32),
            jax.ShapeDtypeStruct((mic_dev, panel_dev), BF16),
        ),
        in_specs=[pl.BlockSpec(memory_space=pltpu.SMEM)] * 2 + [pl.BlockSpec(memory_space=pltpu.VMEM)],
        out_specs=(pl.BlockSpec(memory_space=pltpu.SMEM), pl.BlockSpec(memory_space=pltpu.VMEM)),
    )(delay_groups, patch_block, transfer_matrix)
    return pl.pallas_call(
        body,
        out_shape=jax.ShapeDtypeStruct((PATCH, nvec, half), BF16),
        in_specs=[pl.BlockSpec(memory_space=pltpu.SMEM)] + [pl.BlockSpec(memory_space=pl.ANY)] * 2,
        out_specs=pl.BlockSpec(memory_space=pltpu.VMEM),
        scratch_shapes=scratch,
        compiler_params=pltpu.CompilerParams(
            collective_id=0, has_side_effects=True, vmem_limit_bytes=56 * 1024 * 1024
        ),
    )(delays, sources, tiles)


def solution(mesh):
    placed = (P("panel", None, "tm"), P("mic", "panel"), P("panel", "mic"), P("panel"))
    return jax.shard_map(
        per_device,
        mesh=mesh,
        in_specs=placed,
        out_specs=P(("panel", "mic"), None, "tm"),
        check_vma=False,
    )
```

```python
import jax
import jax.numpy as jnp
from jax import lax
from jax.experimental import pallas as pl
from jax.experimental.pallas import tpu as pltpu
from jax.sharding import PartitionSpec as P

DMAX = 32
PATCH = 128
MB = 128
NVEC = 8
NZ = 8
NX = 4
NCH = 8
CH = 16
ROWS = CH // NZ
OVER = DMAX // CH
MESH = pl.DeviceIdType.MESH
F32 = jnp.float32
BF16 = jnp.bfloat16
ORDER = (
    ("v", 0), ("f", 0), ("s", 0), ("s", 1), ("f", 1), ("s", 2), ("s", 3), ("f", 2), ("s", 4), ("s", 5),
    ("f", 3), ("t", 0), ("t", 1), ("t", 2), ("t", 3), ("m", 0), ("s", 6), ("s", 7), ("t", 4), ("t", 5),
    ("o", 0), ("o", 1), ("o", 2), ("o", 3), ("t", 6), ("t", 7), ("g", 0), ("g", 1), ("o", 4), ("g", 2),
    ("o", 5), ("g", 3), ("o", 6), ("o", 7), ("h", 0), ("g", 4), ("g", 5), ("h", 1), ("h", 2), ("g", 6),
    ("h", 3), ("g", 7), ("w", 0), ("h", 4), ("h", 5), ("w", 1), ("w", 2), ("b", 0), ("d", 0), ("h", 6),
    ("w", 3), ("b", 1), ("d", 1), ("h", 7), ("x", 0), ("w", 4), ("b", 2), ("d", 2), ("w", 5), ("b", 3),
    ("x", 1), ("d", 3), ("w", 6), ("b", 4), ("d", 4), ("x", 2), ("w", 7), ("b", 5), ("d", 5), ("e", 0),
    ("x", 3), ("e", 1), ("x", 4), ("k", 0), ("x", 5), ("b", 6), ("b", 7), ("d", 6), ("d", 7), ("e", 2),
    ("e", 3), ("e", 4), ("x", 6), ("x", 7), ("e", 5), ("e", 6), ("e", 7),
)


def reorder(dg_ref, pb_ref, mat, delays, tiles):
    patches, blocks = dg_ref.shape
    base = lax.axis_index("panel") * patches
    for j in range(patches):
        owner = jnp.int32(0)
        for q in range(patches):
            owner = owner + jnp.where(pb_ref[q] - base == j, q, 0)
        for b in range(blocks):
            delays[j * blocks + b] = dg_ref[owner, b]
        cols = pl.ds(pl.multiple_of(owner * PATCH, PATCH), PATCH)
        tiles[:, j * PATCH : (j + 1) * PATCH] = mat[:, cols]


def body(
    delays, src_hbm, mat_hbm, out_ref,
    sbuf, tiles, fa, fb, st, part, o_part, o_recv, r_half, r_recv, r_send, y_send, y_recv, gath, o_gath, work,
    g_send, g_keep, g_recv, x_send, x_recv, fin,
    in_sem, r_ss, r_rs, y_ss, y_rs, o_ss, o_rs, a_ss, a_rs, b_ss, b_rs, c_ss, c_rs, x_ss, x_rs,
):
    panel_dev, nvec, half = sbuf.shape
    patches = panel_dev // PATCH
    blocks = tiles.shape[0] // MB
    panel, mic, tm = (lax.axis_index(name) for name in ("panel", "mic", "tm"))
    z, y_hi = panel // 2, panel % 2
    x, core = mic // 2, mic % 2

    def z_at(step):
        return (z + step + NZ) % NZ

    def x_at(step):
        return (x + step + NX) % NX

    def z_peer(step):
        return {"panel": z_at(step) * 2 + y_hi}

    def x_peer(step):
        return {"mic": x_at(step) * 2 + core}

    y_peer = {"panel": z * 2 + 1 - y_hi}
    t_peer = {"tm": 1 - tm}
    core_peer = {"mic": x * 2 + 1 - core}
    signs = (1, -1)
    hops = (1, -1, 2)

    barrier = pltpu.get_barrier_semaphore()
    peers = [z_peer(k) for k in (1, -1, 2, -2)] + [y_peer, t_peer, core_peer] + [x_peer(k) for k in hops]
    for peer in peers:
        pl.semaphore_signal(barrier, inc=1, device_id=peer, device_id_type=MESH)

    def load_src(j):
        return pltpu.make_async_copy(
            src_hbm.at[pl.ds(j * PATCH, PATCH)], sbuf.at[pl.ds(j * PATCH, PATCH)], in_sem.at[j]
        )

    load_mat = pltpu.make_async_copy(mat_hbm, tiles, in_sem.at[patches])
    for j in range(patches):
        load_src(j).start()
    load_mat.start()

    st[0:DMAX] = jnp.zeros((DMAX,) + st.shape[1:], st.dtype)
    st[half + DMAX : half + 2 * DMAX] = jnp.zeros((DMAX,) + st.shape[1:], st.dtype)
    work[half : half + DMAX] = jnp.zeros((DMAX,) + work.shape[1:], work.dtype)

    @pl.loop(0, patches)
    def _(j):
        load_src(j).wait()
        fa[...] = sbuf[pl.ds(j * PATCH, PATCH)].astype(F32).reshape(PATCH * nvec, half)
        for n in range(nvec):
            fb[pl.ds(n, half, stride=nvec), :] = fa[pl.ds(n, PATCH, stride=nvec), :].T
        st[DMAX : DMAX + half, :, pl.ds(pl.multiple_of(j * PATCH, PATCH), PATCH)] = (
            fb[...].reshape(half, nvec, PATCH).astype(st.dtype)
        )

    load_mat.wait()
    pl.semaphore_wait(barrier, len(peers))

    def send(source, target, send_sem, recv_sem, peer):
        return pltpu.make_async_remote_copy(
            src_ref=source, dst_ref=target, send_sem=send_sem, recv_sem=recv_sem, device_id=peer, device_id_type=MESH
        )

    def chunk(p):
        return NCH - 1 - p

    def r_copy(kind, way, p):
        sign, c = signs[way], chunk(p)
        sems = r_ss.at[kind, way, p], r_rs.at[kind, way, p]
        if kind == 0:
            return send(part.at[c, z_at(4), pl.ds(way, 1)], r_half.at[way, p], *sems, z_peer(2 * sign))
        if kind == 3:
            return send(r_send.at[way, p], r_recv.at[2, way, p], *sems, z_peer(2 * sign))
        source = part.at[c, z_at(3 * sign if kind == 1 else sign)]
        return send(source, r_recv.at[kind - 1, way, p], *sems, z_peer(sign))

    def y_copy(p):
        return send(y_send.at[p], y_recv.at[p], y_ss.at[p], y_rs.at[p], y_peer)

    def a_copy(kind, way, p):
        sign = signs[way]
        ref = gath.at[p, z] if kind < 2 else gath.at[p, z_at(-2 * sign)]
        if kind == 3:
            ref = gath.at[p, z_at(-2 * sign), pl.ds(way, 1)]
        return send(ref, ref, a_ss.at[kind, way, p], a_rs.at[kind, way, p], z_peer(sign if kind in (0, 2) else 2 * sign))

    def b_copy(step, p):
        k = p - (NCH - OVER)
        return send(
            gath.at[p, z_at(step)], o_gath.at[k, z_at(step)], b_ss.at[step + 3, k], b_rs.at[step + 3, k], t_peer
        )

    def b_start(p, steps):
        if p >= NCH - OVER:

            @pl.when(tm == 1)
            def _():
                for step in steps:
                    b_copy(step, p).start()

    o_copy = send(o_part, o_recv, o_ss, o_rs, t_peer)

    def core_copy(q):
        return send(g_send.at[q], g_recv.at[q], c_ss.at[q], c_rs.at[q], core_peer)

    def x_copy(k, q):
        return send(x_send.at[k, q], x_recv.at[k, q], x_ss.at[k, q], x_rs.at[k, q], x_peer(hops[k]))

    def pressures(first, rows, put):
        for b in range(blocks):
            pieces = []
            for j in range(patches):
                at = pl.ds(first + DMAX - delays[j * blocks + b], rows)
                pieces.append(st[at, :, j * PATCH : (j + 1) * PATCH].reshape(rows * nvec, PATCH))
            acc = lax.dot_general(
                jnp.concatenate(pieces, axis=1), tiles[b * MB : (b + 1) * MB, :],
                (((1,), (1,)), ((), ())), preferred_element_type=F32,
            )
            put(b, acc.astype(BF16))

    def overlap(_):
        @pl.when(tm == 0)
        def _():
            def put(b, value):
                o_part[:, :, b * MB : (b + 1) * MB] = value.reshape(DMAX, nvec, MB)

            pressures(half, DMAX, put)
            o_copy.start()

    def forward(i):
        c = NCH - 2 - 2 * i

        def put(b, value):
            part[c : c + 2, :, :, :, b * MB : (b + 1) * MB] = value.reshape(2, NZ, ROWS, nvec, MB)

        pressures(c * CH, 2 * CH, put)

    def add_overlap(_):
        @pl.when(tm == 1)
        def _():
            o_copy.wait_recv()
            part[0:OVER] = (
                part[0:OVER].astype(F32) + o_recv[...].reshape(OVER, NZ, ROWS, nvec, blocks * MB).astype(F32)
            ).astype(BF16)

    def reduce_first(p):
        for kind in range(3):
            for way in range(2):
                r_copy(kind, way, p).start()

    def reduce_second(p):
        for way in range(2):
            r_copy(0, way, p).wait_recv()
            r_copy(1, way, p).wait_recv()
            dest = z_at(2 * signs[way])
            total = part[chunk(p), dest].astype(F32) + r_recv[0, way, p].astype(F32)
            r_send[way, p, 1 - way] = total[1 - way].astype(BF16)
            r_send[way, p, way] = (total[way] + r_half[way, p, 0].astype(F32)).astype(BF16)
            r_copy(3, way, p).start()

    def own_sum(p):
        total = part[chunk(p), z].astype(F32)
        for kind in (1, 2):
            for way in range(2):
                total = total + r_recv[kind, way, p].astype(F32)
        return total

    def reduce_last(p):
        for way in range(2):
            r_copy(2, way, p).wait_recv()
            r_copy(3, way, p).wait_recv()
        y_send[p] = own_sum(p).astype(BF16)
        y_copy(p).start()

    def gather_first(p):
        y_copy(p).wait_recv()
        gath[p, z] = (own_sum(p) + y_recv[p].astype(F32)).astype(BF16)
        for kind in (1, 0):
            for way in range(2):
                a_copy(kind, way, p).start()
        b_start(p, (0,))

    def gather_second(p):
        for way in range(2):
            a_copy(1, way, p).wait_recv()
            for kind in (3, 2):
                a_copy(kind, way, p).start()
        for way in range(2):
            a_copy(0, way, p).wait_recv()
        b_start(p, (1, -1, 2, -2))

    def gather_last(p):
        for way in range(2):
            a_copy(2, way, p).wait_recv()
            a_copy(3, way, p).wait_recv()
        b_start(p, (3, -3, 4))
        c = chunk(p)
        work[c * CH : (c + 1) * CH] = gath[p].reshape(CH, nvec, blocks * MB)

    def take_overlap(_):
        @pl.when(tm == 0)
        def _():
            for p in range(NCH - OVER, NCH):
                for step in range(-3, 5):
                    b_copy(step, p).wait_recv()
                first = half + chunk(p) * CH
                work[first : first + CH] = o_gath[p - (NCH - OVER)].reshape(CH, nvec, blocks * MB)

    def out_chunk(q):
        return jnp.where(tm == 0, (NCH - 1 - OVER - q) % NCH, NCH - 1 - q)

    def products(q, target, side):
        start = out_chunk(q) * CH
        for k in range(NX):
            j = 2 * k + side
            pieces = []
            for b in range(blocks):
                at = pl.ds(start + delays[j * blocks + b], CH)
                pieces.append(work[at, :, b * MB : (b + 1) * MB].reshape(CH * nvec, MB))
            acc = jnp.dot(
                jnp.concatenate(pieces, axis=1), tiles[:, pl.ds(pl.multiple_of(j * PATCH, PATCH), PATCH)],
                preferred_element_type=F32,
            )
            target[q, k] = acc.reshape(CH, nvec, PATCH).astype(BF16)

    def backward_away(q):
        products(q, g_send, 1 - core)
        core_copy(q).start()

    def backward_own(q):
        products(q, g_keep, core)

    def pair(q, dest):
        return g_keep[q, dest].astype(F32) + g_recv[q, dest].astype(F32)

    def scatter(q):
        core_copy(q).wait_recv()
        for k in (2, 0, 1):
            x_send[k, q] = pair(q, x_at(hops[k])).astype(BF16)
            x_copy(k, q).start()

    def scatter_last(q):
        total = pair(q, x)
        for k in range(3):
            x_copy(k, q).wait_recv()
            total = total + x_recv[k, q].astype(F32)
        fin[pl.ds(out_chunk(q) * CH * nvec, CH * nvec), :] = total.reshape(CH * nvec, PATCH)

    steps = {
        "v": overlap, "f": forward, "m": add_overlap, "s": reduce_first, "t": reduce_second, "o": reduce_last,
        "g": gather_first, "h": gather_second, "w": gather_last, "k": take_overlap,
        "b": backward_away, "d": backward_own, "x": scatter, "e": scatter_last,
    }
    for letter, place in ORDER:
        steps[letter](place)

    for n in range(nvec):
        fb[pl.ds(n, PATCH, stride=nvec), :] = fin[pl.ds(n, half, stride=nvec), :].T
    out_ref[...] = fb[...].reshape(PATCH, nvec, half).astype(BF16)

    @pl.when(tm == 0)
    def _():
        o_copy.wait_send()

    @pl.when(tm == 1)
    def _():
        for p in range(NCH - OVER, NCH):
            for step in range(-3, 5):
                b_copy(step, p).wait_send()

    for p in range(NCH):
        y_copy(p).wait_send()
        core_copy(p).wait_send()
        for k in range(3):
            x_copy(k, p).wait_send()
        for kind in range(4):
            for way in range(2):
                r_copy(kind, way, p).wait_send()
                a_copy(kind, way, p).wait_send()


def per_device(sources, transfer_matrix, delay_groups, patch_block):
    panel_dev, nvec, half = sources.shape
    mic_dev = transfer_matrix.shape[0]
    patches, blocks = delay_groups.shape
    vm = pltpu.VMEM
    dma = pltpu.SemaphoreType.DMA
    own = (ROWS, nvec, mic_dev)
    scratch = [
        vm((panel_dev, nvec, half), BF16),
        vm((mic_dev, panel_dev), BF16),
        vm((PATCH * nvec, half), F32),
        vm((half * nvec, PATCH), F32),
        vm((half + 2 * DMAX, nvec, panel_dev), BF16),
        vm((NCH, NZ) + own, BF16),
        vm((DMAX, nvec, mic_dev), BF16),
        vm((DMAX, nvec, mic_dev), BF16),
        vm((2, NCH, 1, nvec, mic_dev), BF16),
        vm((3, 2, NCH) + own, BF16),
        vm((2, NCH) + own, BF16),
        vm((NCH,) + own, BF16),
        vm((NCH,) + own, BF16),
        vm((NCH, NZ) + own, BF16),
        vm((OVER, NZ) + own, BF16),
        vm((half + DMAX, nvec, mic_dev), BF16),
        vm((NCH, NX, CH, nvec, PATCH), BF16),
        vm((NCH, NX, CH, nvec, PATCH), BF16),
        vm((NCH, NX, CH, nvec, PATCH), BF16),
        vm((3, NCH, CH, nvec, PATCH), BF16),
        vm((3, NCH, CH, nvec, PATCH), BF16),
        vm((half * nvec, PATCH), F32),
        dma((patches + 1,)),
        dma((4, 2, NCH)), dma((4, 2, NCH)),
        dma((NCH,)), dma((NCH,)),
        dma, dma,
        dma((4, 2, NCH)), dma((4, 2, NCH)),
        dma((NZ, OVER)), dma((NZ, OVER)),
        dma((NCH,)), dma((NCH,)),
        dma((3, NCH)), dma((3, NCH)),
    ]
    delays, tiles = pl.pallas_call(
        reorder,
        out_shape=(
            jax.ShapeDtypeStruct((patches * blocks,), jnp.int32),
            jax.ShapeDtypeStruct((mic_dev, panel_dev), BF16),
        ),
        in_specs=[pl.BlockSpec(memory_space=pltpu.SMEM)] * 2 + [pl.BlockSpec(memory_space=pltpu.VMEM)],
        out_specs=(pl.BlockSpec(memory_space=pltpu.SMEM), pl.BlockSpec(memory_space=pltpu.VMEM)),
    )(delay_groups, patch_block, transfer_matrix)
    return pl.pallas_call(
        body,
        out_shape=jax.ShapeDtypeStruct((PATCH, nvec, half), BF16),
        in_specs=[pl.BlockSpec(memory_space=pltpu.SMEM)] + [pl.BlockSpec(memory_space=pl.ANY)] * 2,
        out_specs=pl.BlockSpec(memory_space=pltpu.VMEM),
        scratch_shapes=scratch,
        compiler_params=pltpu.CompilerParams(
            collective_id=0, has_side_effects=True, vmem_limit_bytes=56 * 1024 * 1024
        ),
    )(delays, sources, tiles)


def solution(mesh):
    placed = (P("panel", None, "tm"), P("mic", "panel"), P("panel", "mic"), P("panel"))
    return jax.shard_map(
        per_device,
        mesh=mesh,
        in_specs=placed,
        out_specs=P(("panel", "mic"), None, "tm"),
        check_vma=False,
    )
```

```python
import jax
import jax.numpy as jnp
from jax import lax
from jax.experimental import pallas as pl
from jax.experimental.pallas import tpu as pltpu
from jax.sharding import PartitionSpec as P

DMAX = 32
PATCH = 128
MB = 128
NVEC = 8
NZ = 8
NX = 4
NCH = 8
CH = 16
ROWS = CH // NZ
OVER = DMAX // CH
MESH = pl.DeviceIdType.MESH
F32 = jnp.float32
BF16 = jnp.bfloat16
ORDER = (
    ("v", 0), ("f", 0), ("s", 0), ("s", 1), ("f", 1), ("s", 2), ("s", 3), ("f", 2), ("s", 4), ("s", 5),
    ("f", 3), ("t", 0), ("t", 1), ("t", 2), ("t", 3), ("m", 0), ("s", 6), ("s", 7), ("t", 4), ("t", 5),
    ("o", 0), ("o", 1), ("o", 2), ("o", 3), ("t", 6), ("t", 7), ("g", 0), ("g", 1), ("o", 4), ("g", 2),
    ("o", 5), ("g", 3), ("o", 6), ("o", 7), ("h", 0), ("g", 4), ("g", 5), ("h", 1), ("h", 2), ("g", 6),
    ("h", 3), ("g", 7), ("w", 0), ("h", 4), ("h", 5), ("w", 1), ("w", 2), ("b", 0), ("d", 0), ("h", 6),
    ("w", 3), ("b", 1), ("d", 1), ("h", 7), ("x", 0), ("w", 4), ("b", 2), ("d", 2), ("w", 5), ("b", 3),
    ("x", 1), ("d", 3), ("w", 6), ("b", 4), ("d", 4), ("x", 2), ("w", 7), ("b", 5), ("d", 5), ("e", 0),
    ("x", 3), ("e", 1), ("x", 4), ("k", 0), ("x", 5), ("b", 6), ("b", 7), ("d", 6), ("d", 7), ("e", 2),
    ("e", 3), ("e", 4), ("x", 6), ("x", 7), ("e", 5), ("e", 6), ("e", 7),
)


def body(
    dg_ref, pb_ref, src_hbm, mat_hbm, out_ref,
    sbuf, mat, tiles, fa, fb, st, part, o_part, o_recv, r_half, r_recv, r_send, y_send, y_recv, gath, o_gath, work,
    g_send, g_keep, g_recv, x_send, x_recv, fin, delays,
    in_sem, r_ss, r_rs, y_ss, y_rs, o_ss, o_rs, a_ss, a_rs, b_ss, b_rs, c_ss, c_rs, x_ss, x_rs,
):
    panel_dev, nvec, half = sbuf.shape
    patches = panel_dev // PATCH
    blocks = tiles.shape[0] // MB
    panel, mic, tm = (lax.axis_index(name) for name in ("panel", "mic", "tm"))
    z, y_hi = panel // 2, panel % 2
    x, core = mic // 2, mic % 2

    def z_at(step):
        return (z + step + NZ) % NZ

    def x_at(step):
        return (x + step + NX) % NX

    def z_peer(step):
        return {"panel": z_at(step) * 2 + y_hi}

    def x_peer(step):
        return {"mic": x_at(step) * 2 + core}

    y_peer = {"panel": z * 2 + 1 - y_hi}
    t_peer = {"tm": 1 - tm}
    core_peer = {"mic": x * 2 + 1 - core}
    signs = (1, -1)
    hops = (1, -1, 2)

    barrier = pltpu.get_barrier_semaphore()
    peers = [z_peer(k) for k in (1, -1, 2, -2)] + [y_peer, t_peer, core_peer] + [x_peer(k) for k in hops]
    for peer in peers:
        pl.semaphore_signal(barrier, inc=1, device_id=peer, device_id_type=MESH)

    def load_src(j):
        return pltpu.make_async_copy(
            src_hbm.at[pl.ds(j * PATCH, PATCH)], sbuf.at[pl.ds(j * PATCH, PATCH)], in_sem.at[j]
        )

    load_mat = pltpu.make_async_copy(mat_hbm, mat, in_sem.at[patches])
    for j in range(patches):
        load_src(j).start()
    load_mat.start()

    names = []
    for j in range(patches):
        apart = [pb_ref[q] - panel * patches - j for q in range(patches)]
        names.append([1 - jnp.minimum(gap * gap, 1) for gap in apart])
    for j in range(patches):
        for b in range(blocks):
            total = names[j][0] * dg_ref[b, 0]
            for q in range(1, patches):
                total = total + names[j][q] * dg_ref[b, q]
            delays[j * blocks + b] = total

    st[0:DMAX] = jnp.zeros((DMAX,) + st.shape[1:], st.dtype)
    st[half + DMAX : half + 2 * DMAX] = jnp.zeros((DMAX,) + st.shape[1:], st.dtype)
    work[half : half + DMAX] = jnp.zeros((DMAX,) + work.shape[1:], work.dtype)

    @pl.loop(0, patches)
    def _(j):
        load_src(j).wait()
        fa[...] = sbuf[pl.ds(j * PATCH, PATCH)].astype(F32).reshape(PATCH * nvec, half)
        for n in range(nvec):
            fb[pl.ds(n, half, stride=nvec), :] = fa[pl.ds(n, PATCH, stride=nvec), :].T
        st[DMAX : DMAX + half, :, pl.ds(pl.multiple_of(j * PATCH, PATCH), PATCH)] = (
            fb[...].reshape(half, nvec, PATCH).astype(st.dtype)
        )

    load_mat.wait()
    for j in range(patches):
        weights = [names[j][q].astype(F32) for q in range(patches)]

        @pl.loop(0, mat.shape[0] // 64)
        def _(i):
            rows = pl.ds(pl.multiple_of(i * 64, 64), 64)
            total = weights[0] * mat[rows, 0:PATCH].astype(F32)
            for q in range(1, patches):
                total = total + weights[q] * mat[rows, q * PATCH : (q + 1) * PATCH].astype(F32)
            tiles[rows, j * PATCH : (j + 1) * PATCH] = total.astype(BF16)

    pl.semaphore_wait(barrier, len(peers))

    def send(source, target, send_sem, recv_sem, peer):
        return pltpu.make_async_remote_copy(
            src_ref=source, dst_ref=target, send_sem=send_sem, recv_sem=recv_sem, device_id=peer, device_id_type=MESH
        )

    def chunk(p):
        return NCH - 1 - p

    def r_copy(kind, way, p):
        sign, c = signs[way], chunk(p)
        sems = r_ss.at[kind, way, p], r_rs.at[kind, way, p]
        if kind == 0:
            return send(part.at[c, z_at(4), pl.ds(way, 1)], r_half.at[way, p], *sems, z_peer(2 * sign))
        if kind == 3:
            return send(r_send.at[way, p], r_recv.at[2, way, p], *sems, z_peer(2 * sign))
        source = part.at[c, z_at(3 * sign if kind == 1 else sign)]
        return send(source, r_recv.at[kind - 1, way, p], *sems, z_peer(sign))

    def y_copy(p):
        return send(y_send.at[p], y_recv.at[p], y_ss.at[p], y_rs.at[p], y_peer)

    def a_copy(kind, way, p):
        sign = signs[way]
        ref = gath.at[p, z] if kind < 2 else gath.at[p, z_at(-2 * sign)]
        if kind == 3:
            ref = gath.at[p, z_at(-2 * sign), pl.ds(way, 1)]
        return send(ref, ref, a_ss.at[kind, way, p], a_rs.at[kind, way, p], z_peer(sign if kind in (0, 2) else 2 * sign))

    def b_copy(step, p):
        k = p - (NCH - OVER)
        return send(
            gath.at[p, z_at(step)], o_gath.at[k, z_at(step)], b_ss.at[step + 3, k], b_rs.at[step + 3, k], t_peer
        )

    def b_start(p, steps):
        if p >= NCH - OVER:

            @pl.when(tm == 1)
            def _():
                for step in steps:
                    b_copy(step, p).start()

    o_copy = send(o_part, o_recv, o_ss, o_rs, t_peer)

    def core_copy(q):
        return send(g_send.at[q], g_recv.at[q], c_ss.at[q], c_rs.at[q], core_peer)

    def x_copy(k, q):
        return send(x_send.at[k, q], x_recv.at[k, q], x_ss.at[k, q], x_rs.at[k, q], x_peer(hops[k]))

    def pressures(first, rows, put):
        for b in range(blocks):
            pieces = []
            for j in range(patches):
                at = pl.ds(first + DMAX - delays[j * blocks + b], rows)
                pieces.append(st[at, :, j * PATCH : (j + 1) * PATCH].reshape(rows * nvec, PATCH))
            acc = lax.dot_general(
                jnp.concatenate(pieces, axis=1), tiles[b * MB : (b + 1) * MB, :],
                (((1,), (1,)), ((), ())), preferred_element_type=F32,
            )
            put(b, acc.astype(BF16))

    def overlap(_):
        @pl.when(tm == 0)
        def _():
            def put(b, value):
                o_part[:, :, b * MB : (b + 1) * MB] = value.reshape(DMAX, nvec, MB)

            pressures(half, DMAX, put)
            o_copy.start()

    def forward(i):
        c = NCH - 2 - 2 * i

        def put(b, value):
            part[c : c + 2, :, :, :, b * MB : (b + 1) * MB] = value.reshape(2, NZ, ROWS, nvec, MB)

        pressures(c * CH, 2 * CH, put)

    def add_overlap(_):
        @pl.when(tm == 1)
        def _():
            o_copy.wait_recv()
            part[0:OVER] = (
                part[0:OVER].astype(F32) + o_recv[...].reshape(OVER, NZ, ROWS, nvec, blocks * MB).astype(F32)
            ).astype(BF16)

    def reduce_first(p):
        for kind in range(3):
            for way in range(2):
                r_copy(kind, way, p).start()

    def reduce_second(p):
        for way in range(2):
            r_copy(0, way, p).wait_recv()
            r_copy(1, way, p).wait_recv()
            dest = z_at(2 * signs[way])
            total = part[chunk(p), dest].astype(F32) + r_recv[0, way, p].astype(F32)
            r_send[way, p, 1 - way] = total[1 - way].astype(BF16)
            r_send[way, p, way] = (total[way] + r_half[way, p, 0].astype(F32)).astype(BF16)
            r_copy(3, way, p).start()

    def own_sum(p):
        total = part[chunk(p), z].astype(F32)
        for kind in (1, 2):
            for way in range(2):
                total = total + r_recv[kind, way, p].astype(F32)
        return total

    def reduce_last(p):
        for way in range(2):
            r_copy(2, way, p).wait_recv()
            r_copy(3, way, p).wait_recv()
        y_send[p] = own_sum(p).astype(BF16)
        y_copy(p).start()

    def gather_first(p):
        y_copy(p).wait_recv()
        gath[p, z] = (own_sum(p) + y_recv[p].astype(F32)).astype(BF16)
        for kind in (1, 0):
            for way in range(2):
                a_copy(kind, way, p).start()
        b_start(p, (0,))

    def gather_second(p):
        for way in range(2):
            a_copy(1, way, p).wait_recv()
            for kind in (3, 2):
                a_copy(kind, way, p).start()
        for way in range(2):
            a_copy(0, way, p).wait_recv()
        b_start(p, (1, -1, 2, -2))

    def gather_last(p):
        for way in range(2):
            a_copy(2, way, p).wait_recv()
            a_copy(3, way, p).wait_recv()
        b_start(p, (3, -3, 4))
        c = chunk(p)
        work[c * CH : (c + 1) * CH] = gath[p].reshape(CH, nvec, blocks * MB)

    def take_overlap(_):
        @pl.when(tm == 0)
        def _():
            for p in range(NCH - OVER, NCH):
                for step in range(-3, 5):
                    b_copy(step, p).wait_recv()
                first = half + chunk(p) * CH
                work[first : first + CH] = o_gath[p - (NCH - OVER)].reshape(CH, nvec, blocks * MB)

    def out_chunk(q):
        return jnp.where(tm == 0, (NCH - 1 - OVER - q) % NCH, NCH - 1 - q)

    def products(q, target, side):
        start = out_chunk(q) * CH
        for k in range(NX):
            j = 2 * k + side
            pieces = []
            for b in range(blocks):
                at = pl.ds(start + delays[j * blocks + b], CH)
                pieces.append(work[at, :, b * MB : (b + 1) * MB].reshape(CH * nvec, MB))
            acc = jnp.dot(
                jnp.concatenate(pieces, axis=1), tiles[:, pl.ds(pl.multiple_of(j * PATCH, PATCH), PATCH)],
                preferred_element_type=F32,
            )
            target[q, k] = acc.reshape(CH, nvec, PATCH).astype(BF16)

    def backward_away(q):
        products(q, g_send, 1 - core)
        core_copy(q).start()

    def backward_own(q):
        products(q, g_keep, core)

    def pair(q, dest):
        return g_keep[q, dest].astype(F32) + g_recv[q, dest].astype(F32)

    def scatter(q):
        core_copy(q).wait_recv()
        for k in (2, 0, 1):
            x_send[k, q] = pair(q, x_at(hops[k])).astype(BF16)
            x_copy(k, q).start()

    def scatter_last(q):
        total = pair(q, x)
        for k in range(3):
            x_copy(k, q).wait_recv()
            total = total + x_recv[k, q].astype(F32)
        fin[pl.ds(out_chunk(q) * CH * nvec, CH * nvec), :] = total.reshape(CH * nvec, PATCH)

    steps = {
        "v": overlap, "f": forward, "m": add_overlap, "s": reduce_first, "t": reduce_second, "o": reduce_last,
        "g": gather_first, "h": gather_second, "w": gather_last, "k": take_overlap,
        "b": backward_away, "d": backward_own, "x": scatter, "e": scatter_last,
    }
    for letter, place in ORDER:
        steps[letter](place)

    for n in range(nvec):
        fb[pl.ds(n, PATCH, stride=nvec), :] = fin[pl.ds(n, half, stride=nvec), :].T
    out_ref[...] = fb[...].reshape(PATCH, nvec, half).astype(BF16)

    @pl.when(tm == 0)
    def _():
        o_copy.wait_send()

    @pl.when(tm == 1)
    def _():
        for p in range(NCH - OVER, NCH):
            for step in range(-3, 5):
                b_copy(step, p).wait_send()

    for p in range(NCH):
        y_copy(p).wait_send()
        core_copy(p).wait_send()
        for k in range(3):
            x_copy(k, p).wait_send()
        for kind in range(4):
            for way in range(2):
                r_copy(kind, way, p).wait_send()
                a_copy(kind, way, p).wait_send()


def per_device(sources, transfer_matrix, delay_groups, patch_block):
    panel_dev, nvec, half = sources.shape
    mic_dev = transfer_matrix.shape[0]
    patches, blocks = delay_groups.shape
    vm = pltpu.VMEM
    dma = pltpu.SemaphoreType.DMA
    own = (ROWS, nvec, mic_dev)
    scratch = [
        vm((panel_dev, nvec, half), BF16),
        vm((mic_dev, panel_dev), BF16),
        vm((mic_dev, panel_dev), BF16),
        vm((PATCH * nvec, half), F32),
        vm((half * nvec, PATCH), F32),
        vm((half + 2 * DMAX, nvec, panel_dev), BF16),
        vm((NCH, NZ) + own, BF16),
        vm((DMAX, nvec, mic_dev), BF16),
        vm((DMAX, nvec, mic_dev), BF16),
        vm((2, NCH, 1, nvec, mic_dev), BF16),
        vm((3, 2, NCH) + own, BF16),
        vm((2, NCH) + own, BF16),
        vm((NCH,) + own, BF16),
        vm((NCH,) + own, BF16),
        vm((NCH, NZ) + own, BF16),
        vm((OVER, NZ) + own, BF16),
        vm((half + DMAX, nvec, mic_dev), BF16),
        vm((NCH, NX, CH, nvec, PATCH), BF16),
        vm((NCH, NX, CH, nvec, PATCH), BF16),
        vm((NCH, NX, CH, nvec, PATCH), BF16),
        vm((3, NCH, CH, nvec, PATCH), BF16),
        vm((3, NCH, CH, nvec, PATCH), BF16),
        vm((half * nvec, PATCH), F32),
        pltpu.SMEM((patches * blocks,), jnp.int32),
        dma((patches + 1,)),
        dma((4, 2, NCH)), dma((4, 2, NCH)),
        dma((NCH,)), dma((NCH,)),
        dma, dma,
        dma((4, 2, NCH)), dma((4, 2, NCH)),
        dma((NZ, OVER)), dma((NZ, OVER)),
        dma((NCH,)), dma((NCH,)),
        dma((3, NCH)), dma((3, NCH)),
    ]
    return pl.pallas_call(
        body,
        out_shape=jax.ShapeDtypeStruct((PATCH, nvec, half), BF16),
        in_specs=[pl.BlockSpec(memory_space=pltpu.SMEM)] * 2 + [pl.BlockSpec(memory_space=pl.ANY)] * 2,
        out_specs=pl.BlockSpec(memory_space=pltpu.VMEM),
        scratch_shapes=scratch,
        compiler_params=pltpu.CompilerParams(
            collective_id=0, has_side_effects=True, vmem_limit_bytes=56 * 1024 * 1024
        ),
    )(delay_groups.T, patch_block, sources, transfer_matrix)


def solution(mesh):
    placed = (P("panel", None, "tm"), P("mic", "panel"), P("panel", "mic"), P("panel"))
    return jax.shard_map(
        per_device,
        mesh=mesh,
        in_specs=placed,
        out_specs=P(("panel", "mic"), None, "tm"),
        check_vma=False,
    )
```
